32 devices in a mesh: seq: 2 (over x), fsdp: 16 (over z, y, core).
Axes of the slice: x: 2, y: 2, z: 4, core: 2. Of those that a mesh axis runs over, the one named last changes fastest.
Arguments:
- tokens: bfloat16 [4096, 1024], P(('fsdp', 'seq')), may hold values from -6 to 6
- cotangent: bfloat16 [4096, 1024], P(('fsdp', 'seq')), may hold values from -6 to 6
- documents: int32 [16, 256], P('fsdp'), may hold values from 0 to 3, never falling along the last dimension, each value on 1 to 128 neighbouring positions
- in_weight: bfloat16 [1024, 4384], P('fsdp'), may hold values from -0.1875 to 0.1875
- kernel_taps: float32 [4, 2304], replicated, may hold values from -3 to 3
- kernel_bias: float32 [2304], replicated, may hold values from -0.5 to 0.5
- step_bias: float32 [32], replicated, may hold values from -6 to -2
- decay_log: float32 [32], replicated, may hold values from 0 to 2.77
- skip_gain: float32 [32], replicated, may hold values from 0.5 to 1.5
- pre_gain: float32 [1024], replicated, may hold values from 0.5 to 1.5
- norm_gain: float32 [2048], replicated, may hold values from 0.5 to 1.5
- out_weight: bfloat16 [2048, 1024], P('fsdp'), may hold values from -0.125 to 0.125
Outputs:
- block_output: bfloat16 [4096, 1024], P(('fsdp', 'seq'))
- tokens_grad: float32 [4096, 1024], P(('fsdp', 'seq'))
- in_weight_grad: float32 [1024, 4384], P('fsdp')
- kernel_taps_grad: float32 [4, 2304], replicated
- kernel_bias_grad: float32 [2304], replicated
- step_bias_grad: float32 [32], replicated
- decay_log_grad: float32 [32], replicated
- skip_gain_grad: float32 [32], replicated
- pre_gain_grad: float32 [1024], replicated
- norm_gain_grad: float32 [2048], replicated
- out_weight_grad: float32 [2048, 1024], P('fsdp')
The draws below stay inside these ranges and needn't reach their ends.
Inputs may be any that keep to these rules, and one draw needn't show every extreme that they name: `documents`: in every sequence the ids start at 0 and never fall; each id marks one document of consecutive tokens, and every id of 0 to 3 occurs.
All inputs are finite; a program needn't handle non-finite values.
Results may differ from the reference program's by a relative error of at most 0.011.
Values may be sent and summed in bfloat16 or wider, within the bound.
A program may use at most 128 MiB of HBM per device.

```python
import math
from functools import partial
import jax
import jax.numpy as jnp
import numpy as np
from jax import lax

D = 1024
HEADS = 32
HEAD_DIM = 64
STATE = 128
CONV = 4
SPAN = 256
DOCS = 4
INNER = 2048
CONV_CH = 2304
PROJ = 4384
SEQ_LEN = 256
SEQS = 16
TOKENS = 4096


def shard_levels(stream_key, extent, pieces, least, high):
    factor_of, own = 1.0, jax.random.fold_in(stream_key, 6)
    for axis_at, blocks in pieces:
        steps = jnp.exp(jax.random.uniform(jax.random.fold_in(own, axis_at), (blocks,), jnp.float32, least / len(pieces), high / len(pieces)))
        factor_of = factor_of * jnp.repeat(steps, extent[axis_at] // blocks).reshape([-1 if axis == axis_at else 1 for axis in range(len(extent))])
    return factor_of


def profile(amount, total, most, lean):
    weights = [(1 << 20) // math.isqrt(standing ** lean) + 1 for standing in range(2, amount + 1)]
    surplus, counts = total - most - (amount - 1), [1] * (amount - 1)
    while surplus > 0:
        free = [i for i in range(amount - 1) if counts[i] < most]
        mass, left = sum([weights[i] for i in free]), surplus
        for i in free:
            extra = min(most - counts[i], max(1, left * weights[i] // mass), surplus)
            counts[i] = counts[i] + extra
            surplus = surplus - extra
    return np.array([most] + counts)


def ragged(rng, number_of, total, most, skew):
    if number_of == 2:
        one = jax.random.randint(rng, (), max(1, total - most), min(most, total - 1) + 1)
        return jnp.stack([one, total - one])
    tallies = jnp.asarray(profile(number_of, total, most, skew), jnp.int32)
    twos = (number_of - 1) // 2
    source_of, sink = tallies[1:1 + 2 * twos:2], tallies[2:2 + 2 * twos:2]
    room = jnp.minimum(source_of - 1, most - sink)
    moved = jax.random.randint(jax.random.fold_in(rng, 1), (twos,), 0, 1 << 20) % (room + 1)
    tallies = tallies.at[1:1 + 2 * twos:2].set(source_of - moved).at[2:2 + 2 * twos:2].set(sink + moved)
    return tallies[jax.random.permutation(jax.random.fold_in(rng, 2), number_of)]


def normal_values(rng, shape, spread, reach, pieces=(), kind=jnp.bfloat16):
    drawn = jax.random.normal(rng, shape, jnp.float32) * spread
    if len(pieces) > 0:
        drawn = shard_levels(rng, shape, pieces, -0.22, 0.18) * drawn
    return jnp.clip(drawn, min=-reach, max=reach).astype(kind)


def setup_inputs(seed: int = 0) -> dict:
    key_of = jax.random.split(jax.random.key(seed), 13)
    return {
        "tokens": normal_values(key_of[0], (TOKENS, D), 1.0, 6.0, ((0, 32),)),
        "cotangent": normal_values(key_of[1], (TOKENS, D), 1.0, 6.0, ((0, 32),)),
        "documents": jax.vmap(lambda own: jnp.searchsorted(jnp.cumsum(ragged(own, DOCS, SEQ_LEN, SEQ_LEN // 2, 1)), jnp.arange(SEQ_LEN), side="right"))(jax.random.split(key_of[2], SEQS)).reshape((SEQS, SEQ_LEN)).astype(jnp.int32),
        "in_weight": normal_values(key_of[3], (D, PROJ), D ** -0.5, 0.1875, ((0, 16),)),
        "kernel_taps": normal_values(key_of[4], (CONV, CONV_CH), CONV ** -0.5, 3.0, (), jnp.float32),
        "kernel_bias": jnp.clip(jax.random.uniform(key_of[5], (CONV_CH,), jnp.float32, -0.5, 0.5), -0.5, 0.5),
        "step_bias": jnp.clip(jax.random.uniform(key_of[6], (HEADS,), jnp.float32, -6.0, -2.0), -6.0, -2.0),
        "decay_log": jnp.clip(jax.random.uniform(key_of[7], (HEADS,), jnp.float32, 0.0, 2.77), 0.0, 2.77),
        "skip_gain": jnp.clip(jax.random.uniform(key_of[8], (HEADS,), jnp.float32, 0.5, 1.5), 0.5, 1.5),
        "pre_gain": jnp.clip(1.0 + 0.1 * jax.random.normal(key_of[9], (D,), jnp.float32), 0.5, 1.5),
        "norm_gain": jnp.clip(1.0 + 0.1 * jax.random.normal(key_of[10], (INNER,), jnp.float32), 0.5, 1.5),
        "out_weight": normal_values(key_of[11], (INNER, D), INNER ** -0.5, 0.125, ((0, 16),)),
    }


norm_epsilon = 1e-05

def pre_norm(values, gain):
    scale = lax.rsqrt(lax.optimization_barrier(jnp.mean(values * values, axis=-1, keepdims=True)) + norm_epsilon)
    return values * scale * gain

def gate_norm(mixed, gates, gain):
    gated = mixed * jax.nn.silu(gates)
    scale = lax.rsqrt(lax.optimization_barrier(jnp.mean(gated * gated, axis=-1, keepdims=True)) + norm_epsilon)
    return gated * scale * gain

def block_step(state, block):
    scaled, input_matrix, output_matrix, log_block, seg_block, prev_last = block
    width = seg_block.shape[0]
    cumul = jnp.cumsum(log_block, axis=0).T
    places = jnp.arange(width)
    causal = (places[:, None] >= places[None, :]) & (seg_block[:, None] == seg_block[None, :])
    log_gap = cumul[:, :, None] - cumul[:, None, :]
    decay = jnp.where(causal[None], jnp.exp(jnp.where(causal[None], log_gap, 0.0)), 0.0)
    scores = jnp.dot(output_matrix, input_matrix.T, precision=lax.Precision.HIGHEST)
    inside = jnp.einsum('hij,jhp->ihp', decay * scores[None], scaled, precision=lax.Precision.HIGHEST)
    entering = jnp.exp(cumul) * (seg_block == prev_last).astype(jnp.float32)[None]
    carried = jnp.einsum('in,hnp->ihp', output_matrix, state, precision=lax.Precision.HIGHEST) * entering.T[:, :, None]
    final = cumul[:, -1]
    leaving = jnp.exp(final[:, None] - cumul) * (seg_block == seg_block[-1]).astype(jnp.float32)[None]
    fresh = jnp.einsum('hj,jn,jhp->hnp', leaving, input_matrix, scaled, precision=lax.Precision.HIGHEST)
    keeping = jnp.exp(final) * (seg_block[-1] == prev_last).astype(jnp.float32)
    new_state = keeping[:, None, None] * state + fresh
    return (new_state, inside + carried)

def mixer(segment, conv_in, step_raw, taps, tap_bias, bias_steps, log_rates, skips):
    length, channels = conv_in.shape
    heads = step_raw.shape[1]
    width = heads * HEAD_DIM
    summed = tap_bias + conv_in * taps[CONV - 1]
    for offset in range(1, CONV):
        shifted = jnp.concatenate([jnp.zeros((offset, channels), jnp.float32), conv_in[:length - offset]], axis=0)
        matched = jnp.concatenate([jnp.zeros((offset,), jnp.float32), (segment[offset:] == segment[:length - offset]).astype(jnp.float32)])
        summed = summed + taps[CONV - 1 - offset] * shifted * matched[:, None]
    active = jax.nn.silu(summed)
    values = active[:, :width].reshape(length, heads, HEAD_DIM)
    input_matrix = active[:, width:width + STATE]
    output_matrix = active[:, width + STATE:]
    steps_taken = jax.nn.softplus(step_raw + bias_steps)
    log_decay = steps_taken * -jnp.exp(log_rates)
    scaled = values * steps_taken[:, :, None]
    blocks = length // SPAN
    seg_blocks = segment.reshape(blocks, SPAN)
    prev_last = jnp.concatenate([seg_blocks[:1, 0], seg_blocks[:-1, -1]])
    initial = jnp.zeros((heads, STATE, HEAD_DIM), jnp.float32)
    _, outputs = lax.scan(block_step, initial, (scaled.reshape(blocks, SPAN, heads, HEAD_DIM), input_matrix.reshape(blocks, SPAN, STATE), output_matrix.reshape(blocks, SPAN, STATE), log_decay.reshape(blocks, SPAN, heads), seg_blocks, prev_last))
    result = outputs.reshape(length, heads, HEAD_DIM) + values * skips[None, :, None]
    return result.reshape(length, width)

def reference(tokens, cotangent, documents, in_weight, kernel_taps, kernel_bias, step_bias, decay_log, skip_gain, pre_gain, norm_gain, out_weight):

    def sequence_pass(carry, inputs):
        tokens_seq, cot_seq, segment = inputs
        floats = tokens_seq.astype(jnp.float32)
        normed_in = pre_norm(floats, pre_gain).astype(jnp.bfloat16)
        projected = jnp.dot(normed_in, in_weight, preferred_element_type=jnp.float32).astype(jnp.bfloat16)
        gates = projected[:, :INNER]
        conv_in = projected[:, INNER:INNER + CONV_CH]
        step_raw = projected[:, INNER + CONV_CH:]
        mixed, mixer_back = jax.vjp(partial(mixer, segment), conv_in.astype(jnp.float32), step_raw.astype(jnp.float32), kernel_taps, kernel_bias, step_bias, decay_log, skip_gain)
        mixed_bf = mixed.astype(jnp.bfloat16)
        normed_out, norm_back = jax.vjp(gate_norm, mixed_bf.astype(jnp.float32), gates.astype(jnp.float32), norm_gain)
        normed_bf = normed_out.astype(jnp.bfloat16)
        branch = jnp.dot(normed_bf, out_weight, preferred_element_type=jnp.float32)
        block_out = (floats + branch).astype(jnp.bfloat16)
        back_normed = jnp.dot(cot_seq, out_weight.T, preferred_element_type=jnp.float32)
        out_grad = jnp.dot(normed_bf.T, cot_seq, preferred_element_type=jnp.float32)
        back_mixed, back_gates, gain_two = norm_back(back_normed)
        back_mixed_bf = back_mixed.astype(jnp.bfloat16)
        grads = mixer_back(back_mixed_bf.astype(jnp.float32))
        back_projected = jnp.concatenate([back_gates.astype(jnp.bfloat16), grads[0].astype(jnp.bfloat16), grads[1].astype(jnp.bfloat16)], axis=1)
        back_normed_in = jnp.dot(back_projected, in_weight.T, preferred_element_type=jnp.float32)
        in_grad = jnp.dot(normed_in.T, back_projected, preferred_element_type=jnp.float32)
        _, pre_back = jax.vjp(pre_norm, floats, pre_gain)
        back_floats, gain_one = pre_back(back_normed_in)
        token_grad = cot_seq.astype(jnp.float32) + back_floats
        updates = (in_grad, grads[2], grads[3], grads[4], grads[5], grads[6], gain_one, gain_two, out_grad)
        carry = tuple((total + part for total, part in zip(carry, updates)))
        return (carry, (block_out, token_grad))
    initial = (jnp.zeros((D, PROJ), jnp.float32), jnp.zeros((CONV, CONV_CH), jnp.float32), jnp.zeros((CONV_CH,), jnp.float32), jnp.zeros((HEADS,), jnp.float32), jnp.zeros((HEADS,), jnp.float32), jnp.zeros((HEADS,), jnp.float32), jnp.zeros((D,), jnp.float32), jnp.zeros((INNER,), jnp.float32), jnp.zeros((INNER, D), jnp.float32))
    totals, (outputs, token_grads) = lax.scan(sequence_pass, initial, (tokens.reshape(SEQS, SEQ_LEN, D), cotangent.reshape(SEQS, SEQ_LEN, D), documents))
    return (outputs.reshape(TOKENS, D), token_grads.reshape(TOKENS, D), totals[0], totals[1], totals[2], totals[3], totals[4], totals[5], totals[6], totals[7], totals[8])
```

```python
import jax
import jax.numpy as jnp
from jax import lax
from jax.sharding import PartitionSpec as P

HEAD_DIM = 64
STATE = 128
CONV = 4
SPAN = 256

norm_epsilon = 1e-05
bf16 = jnp.bfloat16
f32 = jnp.float32
contract_rows = (((1,), (1,)), ((), ()))
contract_tokens = (((0,), (0,)), ((), ()))


def dot(left, right, dims=(((1,), (0,)), ((), ()))):
    return lax.dot_general(left, right, dims, preferred_element_type=f32)


def pre_norm(values, gain):
    scale = lax.rsqrt(jnp.mean(values * values, axis=-1, keepdims=True) + norm_epsilon)
    return values * scale * gain


def product(spec, left, right):
    return jnp.einsum(spec, left.astype(bf16), right.astype(bf16), preferred_element_type=f32)


def mixer(segment, conv_in, step_raw, taps, tap_bias, bias_steps, log_rates, skips):
    length, channels = conv_in.shape
    heads = step_raw.shape[1]
    width = heads * HEAD_DIM
    summed = tap_bias + conv_in * taps[CONV - 1]
    for offset in range(1, CONV):
        shifted = jnp.concatenate(
            [jnp.zeros((offset, channels), f32), conv_in[: length - offset]], axis=0
        )
        matched = jnp.concatenate(
            [
                jnp.zeros((offset,), f32),
                (segment[offset:] == segment[: length - offset]).astype(f32),
            ]
        )
        summed = summed + taps[CONV - 1 - offset] * shifted * matched[:, None]
    active = jax.nn.silu(summed)
    values = active[:, :width].reshape(length, heads, HEAD_DIM).transpose(1, 0, 2)
    input_matrix = active[:, width : width + STATE]
    output_matrix = active[:, width + STATE :]
    steps_taken = jax.nn.softplus(step_raw + bias_steps)
    log_decay = (steps_taken * -jnp.exp(log_rates)).T
    scaled = values * steps_taken.T[:, :, None]
    span = min(SPAN, length)
    blocks = length // span
    places = jnp.arange(span)
    state = None
    outputs = []
    for block in range(blocks):
        at = slice(block * span, (block + 1) * span)
        seg = segment[at]
        cumul = jnp.cumsum(log_decay[:, at], axis=1)
        causal = (places[:, None] >= places[None, :]) & (seg[:, None] == seg[None, :])
        log_gap = cumul[:, :, None] - cumul[:, None, :]
        decay = jnp.where(causal[None], jnp.exp(jnp.where(causal[None], log_gap, 0.0)), 0.0)
        scores = product("in,jn->ij", output_matrix[at], input_matrix[at])
        inside = product("hij,hjp->hip", decay * scores[None], scaled[:, at])
        if state is not None:
            previous = segment[block * span - 1]
            entering = jnp.exp(cumul) * (seg == previous).astype(f32)[None]
            inside = inside + product("in,hnp->hip", output_matrix[at], state) * entering[:, :, None]
        if block + 1 < blocks:
            final = cumul[:, -1]
            leaving = jnp.exp(final[:, None] - cumul) * (seg == seg[-1]).astype(f32)[None]
            fresh = product("jn,hjp->hnp", input_matrix[at], scaled[:, at] * leaving[:, :, None])
            if state is None:
                state = fresh
            else:
                keeping = jnp.exp(final) * (seg[-1] == previous).astype(f32)
                state = keeping[:, None, None] * state + fresh
        outputs.append(inside)
    whole = outputs[0] if blocks == 1 else jnp.concatenate(outputs, axis=1)
    result = whole + values * skips[:, None, None]
    return result.transpose(1, 0, 2).reshape(length, width)


def local(
    tokens,
    cotangent,
    documents,
    in_weight,
    kernel_taps,
    kernel_bias,
    step_bias,
    decay_log,
    skip_gain,
    pre_gain,
    norm_gain,
    out_weight,
):
    groups = lax.axis_size("seq")
    shards = lax.axis_size("fsdp")
    group = lax.axis_index("seq")
    heads = step_bias.shape[0]
    inner = norm_gain.shape[0]
    states = kernel_bias.shape[0] - inner
    half = inner // groups
    spread = out_weight.shape[0] % (HEAD_DIM * groups) == 0
    parts = shards if spread else 1

    def pick(array, axis):
        size = array.shape[axis]
        lead, tail = array.shape[:axis], array.shape[axis + 1 :]
        split = array.reshape(lead + (parts, groups, size // (parts * groups)) + tail)
        chosen = lax.dynamic_index_in_dim(split, group, axis + 1, keepdims=False)
        return chosen.reshape(lead + (size // groups,) + tail)

    def place(array):
        size = array.shape[-1] * groups
        lead = array.shape[:-1]
        split = array.reshape(lead + (parts, 1, size // (parts * groups)))
        blank = jnp.zeros(lead + (parts, groups, size // (parts * groups)), array.dtype)
        full = lax.dynamic_update_slice_in_dim(blank, split, group, len(lead) + 1)
        return full.reshape(lead + (size,))

    def unite(array):
        rows, width = array.shape[1:]
        split = array.reshape(groups, rows, parts, width // parts)
        return split.transpose(1, 2, 0, 3).reshape(rows, width * groups)

    conv_end = inner + inner + states
    conv_shard = jnp.concatenate(
        [
            pick(in_weight[:, inner : 2 * inner], 1),
            in_weight[:, 2 * inner : conv_end],
            pick(in_weight[:, conv_end:], 1),
        ],
        axis=1,
    )
    conv_weight = lax.all_gather(conv_shard, "fsdp", axis=0, tiled=True)
    gate_shard, conv_weight = lax.optimization_barrier(
        (pick(in_weight[:, :inner], 1), conv_weight)
    )
    gate_weight = lax.all_gather(gate_shard, "fsdp", axis=0, tiled=True)
    out_rows = None
    if spread:
        split = out_weight.reshape(groups, out_weight.shape[0] // groups, out_weight.shape[1])
        out_rows = lax.dynamic_index_in_dim(split, group, 0, keepdims=False)
    else:
        out_rows = out_weight
    out_rows, gate_weight = lax.optimization_barrier((out_rows, gate_weight))
    out_part = lax.all_gather(out_rows, "fsdp", axis=0, tiled=True)
    if not spread:
        out_part = lax.dynamic_slice_in_dim(out_part, group * half, half, 0)

    floats = tokens.astype(f32)
    normed_own = pre_norm(floats, pre_gain).astype(bf16)
    joined = lax.all_gather(
        jnp.concatenate([normed_own, cotangent], axis=1), "seq", axis=0, tiled=True
    )
    width = tokens.shape[1]
    normed_in, cot = joined[:, :width], joined[:, width:]

    projected = dot(normed_in, conv_weight).astype(bf16).astype(f32)
    segment = documents[0]
    taps = jnp.concatenate([pick(kernel_taps[:, :inner], 1), kernel_taps[:, inner:]], axis=1)
    tap_bias = jnp.concatenate([pick(kernel_bias[:inner], 0), kernel_bias[inner:]], axis=0)
    mixed, mixer_back = jax.vjp(
        lambda *given: mixer(segment, *given),
        projected[:, : half + states],
        projected[:, half + states :],
        taps,
        tap_bias,
        pick(step_bias, 0),
        pick(decay_log, 0),
        pick(skip_gain, 0),
    )
    gain = pick(norm_gain, 0)
    gates = dot(normed_in, gate_weight).astype(bf16).astype(f32)
    mixed = mixed.astype(bf16).astype(f32)
    back_normed = dot(cot, out_part, contract_rows)
    sigmoid = jax.nn.sigmoid(gates)
    silu = gates * sigmoid
    gated = mixed * silu
    back_gain = back_normed * gain
    sums = lax.psum(
        jnp.stack([jnp.sum(gated * gated, axis=1), jnp.sum(gated * back_gain, axis=1)]), "seq"
    )
    scale = lax.rsqrt(sums[0] / inner + norm_epsilon)
    unit = gated * scale[:, None]
    normed_bf = (unit * gain).astype(bf16)
    norm_gain_part = jnp.sum(back_normed * unit, axis=0)
    back_gated = scale[:, None] * (back_gain - unit * (scale * sums[1] / inner)[:, None])
    back_mixed = (back_gated * silu).astype(bf16).astype(f32)
    back_gates = (back_gated * mixed * sigmoid * (1.0 + gates * (1.0 - sigmoid))).astype(bf16)

    outward = dot(normed_bf, cot, contract_tokens).astype(bf16)
    gate_grad = dot(normed_in, back_gates, contract_tokens).astype(bf16)
    gate_grad = lax.psum_scatter(gate_grad, "fsdp", scatter_dimension=0, tiled=True)
    if spread:
        outward = lax.psum_scatter(outward, "fsdp", scatter_dimension=0, tiled=True)
        outward_grad = lax.all_gather(outward, "seq", axis=0, tiled=True).astype(f32)
    else:
        blank = jnp.zeros((inner, width), bf16)
        outward = lax.dynamic_update_slice_in_dim(blank, outward, group * half, 0)
        outward = lax.psum_scatter(outward, "fsdp", scatter_dimension=0, tiled=True)
        outward_grad = lax.psum(outward.astype(f32), "seq")
    branch = lax.psum_scatter(
        dot(normed_bf, out_part).astype(bf16), "seq", scatter_dimension=0, tiled=True
    )
    block_output = (floats + branch.astype(f32)).astype(bf16)

    back_conv, back_steps, taps_part, bias_part, step_part, decay_part, skip_part = mixer_back(
        back_mixed
    )
    back_projected = jnp.concatenate([back_conv, back_steps], axis=1).astype(bf16)
    conv_grad = lax.psum_scatter(
        dot(normed_in, back_projected, contract_tokens).astype(bf16),
        "fsdp",
        scatter_dimension=0,
        tiled=True,
    )
    back_in = dot(back_projected, conv_weight, contract_rows) + dot(
        back_gates, gate_weight, contract_rows
    )
    back_in = lax.psum_scatter(back_in.astype(bf16), "seq", scatter_dimension=0, tiled=True)
    _, pre_back = jax.vjp(pre_norm, floats, pre_gain)
    back_floats, pre_gain_part = pre_back(back_in.astype(f32))
    tokens_grad = cotangent.astype(f32) + back_floats

    gate_all = lax.all_gather(gate_grad, "seq", axis=0).astype(f32)
    conv_all = lax.all_gather(conv_grad, "seq", axis=0).astype(f32)
    inward_grad = jnp.concatenate(
        [
            unite(gate_all),
            unite(conv_all[:, :, :half]),
            jnp.sum(conv_all[:, :, half : half + states], axis=0),
            unite(conv_all[:, :, half + states :]),
        ],
        axis=1,
    )

    pieces = (
        jnp.concatenate([place(taps_part[:, :half]), taps_part[:, half:]], axis=1),
        jnp.concatenate([place(bias_part[:half]), bias_part[half:]], axis=0),
        place(step_part),
        place(decay_part),
        place(skip_part),
        pre_gain_part,
        place(norm_gain_part),
    )
    flat = lax.psum(jnp.concatenate([piece.reshape(-1) for piece in pieces]), ("seq", "fsdp"))
    totals = []
    start = 0
    for piece in pieces:
        totals.append(flat[start : start + piece.size].reshape(piece.shape))
        start += piece.size
    return (
        block_output,
        tokens_grad,
        inward_grad,
        totals[0],
        totals[1],
        totals[2],
        totals[3],
        totals[4],
        totals[5],
        totals[6],
        outward_grad,
    )


def solution(mesh):
    rows = P(("fsdp", "seq"), None)
    split = P("fsdp", None)
    return jax.shard_map(
        local,
        mesh=mesh,
        in_specs=(rows, rows, split, split) + (P(),) * 7 + (split,),
        out_specs=(rows, rows, split) + (P(),) * 7 + (split,),
        check_vma=False,
    )
```

```python
import functools
import math

import jax
import jax.numpy as jnp
from jax import lax
from jax.experimental import pallas as pl
from jax.experimental.pallas import tpu as pltpu
from jax.sharding import PartitionSpec as P

HEAD_DIM = 64
STATE = 128
CONV = 4
SPAN = 256

norm_epsilon = 1e-05
bf16 = jnp.bfloat16
f32 = jnp.float32
contract_rows = (((1,), (1,)), ((), ()))
contract_tokens = (((0,), (0,)), ((), ()))


def dot(left, right, dims=(((1,), (0,)), ((), ()))):
    return lax.dot_general(left, right, dims, preferred_element_type=f32)


def pre_norm(values, gain):
    scale = lax.rsqrt(jnp.mean(values * values, axis=-1, keepdims=True) + norm_epsilon)
    return values * scale * gain


def product(spec, left, right):
    return jnp.einsum(spec, left.astype(bf16), right.astype(bf16), preferred_element_type=f32)


def mixer(segment, conv_in, step_raw, taps, tap_bias, bias_steps, log_rates, skips):
    length, channels = conv_in.shape
    heads = step_raw.shape[1]
    width = heads * HEAD_DIM
    summed = tap_bias + conv_in * taps[CONV - 1]
    for offset in range(1, CONV):
        shifted = jnp.concatenate(
            [jnp.zeros((offset, channels), f32), conv_in[: length - offset]], axis=0
        )
        matched = jnp.concatenate(
            [
                jnp.zeros((offset,), f32),
                (segment[offset:] == segment[: length - offset]).astype(f32),
            ]
        )
        summed = summed + taps[CONV - 1 - offset] * shifted * matched[:, None]
    active = jax.nn.silu(summed)
    values = active[:, :width].reshape(length, heads, HEAD_DIM).transpose(1, 0, 2)
    input_matrix = active[:, width : width + STATE]
    output_matrix = active[:, width + STATE :]
    steps_taken = jax.nn.softplus(step_raw + bias_steps)
    log_decay = (steps_taken * -jnp.exp(log_rates)).T
    scaled = values * steps_taken.T[:, :, None]
    span = min(SPAN, length)
    blocks = length // span
    places = jnp.arange(span)
    state = None
    outputs = []
    for block in range(blocks):
        at = slice(block * span, (block + 1) * span)
        seg = segment[at]
        cumul = jnp.cumsum(log_decay[:, at], axis=1)
        causal = (places[:, None] >= places[None, :]) & (seg[:, None] == seg[None, :])
        log_gap = cumul[:, :, None] - cumul[:, None, :]
        decay = jnp.where(causal[None], jnp.exp(jnp.where(causal[None], log_gap, 0.0)), 0.0)
        scores = product("in,jn->ij", output_matrix[at], input_matrix[at])
        inside = product("hij,hjp->hip", decay * scores[None], scaled[:, at])
        if state is not None:
            previous = segment[block * span - 1]
            entering = jnp.exp(cumul) * (seg == previous).astype(f32)[None]
            inside = inside + product("in,hnp->hip", output_matrix[at], state) * entering[:, :, None]
        if block + 1 < blocks:
            final = cumul[:, -1]
            leaving = jnp.exp(final[:, None] - cumul) * (seg == seg[-1]).astype(f32)[None]
            fresh = product("jn,hjp->hnp", input_matrix[at], scaled[:, at] * leaving[:, :, None])
            if state is None:
                state = fresh
            else:
                keeping = jnp.exp(final) * (seg[-1] == previous).astype(f32)
                state = keeping[:, None, None] * state + fresh
        outputs.append(inside)
    whole = outputs[0] if blocks == 1 else jnp.concatenate(outputs, axis=1)
    result = whole + values * skips[:, None, None]
    return result.transpose(1, 0, 2).reshape(length, width)

MESH = pl.DeviceIdType.MESH
VMEM_LIMIT = 60 * 1024 * 1024


def factors(shards):
    rest = shards // 2
    mid = 1 << (int(math.log2(rest)) // 2)
    return rest // mid, mid


def position(top, mid):
    me = lax.axis_index("fsdp")
    return me, me // (2 * mid), lax.rem(me // 2, mid), lax.rem(me, 2)


def slot_of(t, m, core, mid):
    return (t * mid + m) * 2 + core


def greet(groups, top, mid):
    me, t, m, core = position(top, mid)
    group = lax.axis_index("seq")
    peers = [{"fsdp": slot_of(lax.rem(t + d, top), m, core, mid)} for d in range(1, top)]
    peers += [{"fsdp": slot_of(t, lax.rem(m + e, mid), core, mid)} for e in range(1, mid)]
    peers += [{"fsdp": slot_of(t, m, 1 - core, mid)}]
    peers += [{"seq": lax.rem(group + k, groups)} for k in range(1, groups)]
    barrier = pltpu.get_barrier_semaphore()
    for peer in peers:
        pl.semaphore_signal(barrier, inc=1, device_id=peer, device_id_type=MESH)
    pl.semaphore_wait(barrier, len(peers))


def remote(source, target, send, receive, device):
    copy = pltpu.make_async_remote_copy(
        src_ref=source,
        dst_ref=target,
        send_sem=send,
        recv_sem=receive,
        device_id=device,
        device_id_type=MESH,
    )
    copy.start()
    return copy


def gather_kernel(groups, top, mid, count, *refs):
    rows, shards = refs[0], refs[1 : 1 + count]
    all_rows, wholes = refs[1 + count], refs[2 + count : 2 + 2 * count]
    send, receive, row_send, row_receive = refs[2 + 2 * count :]
    me, t, m, core = position(top, mid)
    group = lax.axis_index("seq")
    greet(groups, top, mid)
    copies = {}

    def launch(a, key, source, slot, device):
        copies[(a,) + key] = remote(
            source, wholes[a].at[slot], send.at[(a,) + key], receive.at[(a,) + key], device
        )

    other = {"fsdp": slot_of(t, m, 1 - core, mid)}
    for a in range(count):
        for d in range(1, top):
            peer = {"fsdp": slot_of(lax.rem(t + d, top), m, core, mid)}
            launch(a, (d, 0, 0), shards[a], me, peer)
        for e in range(1, mid):
            peer = {"fsdp": slot_of(t, lax.rem(m + e, mid), core, mid)}
            launch(a, (0, e, 0), shards[a], me, peer)
        launch(a, (0, 0, 1), shards[a], me, other)
    for k in range(1, groups):
        copies[("rows", k)] = remote(
            rows,
            all_rows.at[group],
            row_send.at[k],
            row_receive.at[k],
            {"seq": lax.rem(group + k, groups)},
        )
    for a in range(count):
        wholes[a][me] = shards[a][...]
    all_rows[group] = rows[...]
    for a in range(count):
        for d in range(1, top):
            copies[(a, d, 0, 0)].wait_recv()
            slot = slot_of(lax.rem(t - d + top, top), m, core, mid)
            for e in range(1, mid):
                peer = {"fsdp": slot_of(t, lax.rem(m + e, mid), core, mid)}
                launch(a, (d, e, 0), wholes[a].at[slot], slot, peer)
            launch(a, (d, 0, 1), wholes[a].at[slot], slot, other)
    for a in range(count):
        for d in range(top):
            for e in range(1, mid):
                copies[(a, d, e, 0)].wait_recv()
                slot = slot_of(lax.rem(t - d + top, top), lax.rem(m - e + mid, mid), core, mid)
                launch(a, (d, e, 1), wholes[a].at[slot], slot, other)
    for key, copy in copies.items():
        copy.wait_send()
        if key[0] == "rows" or key[3] == 1:
            copy.wait_recv()


def gather_all(groups, shards, rows, arrays):
    top, mid = factors(shards)
    count = len(arrays)
    vmem = pl.BlockSpec(memory_space=pltpu.VMEM)
    out = [jax.ShapeDtypeStruct((groups,) + rows.shape, rows.dtype)]
    out += [jax.ShapeDtypeStruct((shards,) + array.shape, array.dtype) for array in arrays]
    return pl.pallas_call(
        functools.partial(gather_kernel, groups, top, mid, count),
        out_shape=out,
        in_specs=[vmem] * (1 + count),
        out_specs=[vmem] * (1 + count),
        scratch_shapes=[
            pltpu.SemaphoreType.DMA((count, top, mid, 2)),
            pltpu.SemaphoreType.DMA((count, top, mid, 2)),
            pltpu.SemaphoreType.DMA((groups,)),
            pltpu.SemaphoreType.DMA((groups,)),
        ],
        compiler_params=pltpu.CompilerParams(
            collective_id=0, has_side_effects=True, vmem_limit_bytes=VMEM_LIMIT
        ),
    )(rows, *arrays)


CHUNKS = 2


def add(left, right):
    return (left.astype(f32) + right.astype(f32)).astype(bf16)


def scatter_kernel(groups, top, mid, count, *refs):
    partial, flat, grads = refs[0], refs[1], refs[2 : 2 + count]
    refs = refs[2 + count :]
    summed, total, owned = refs[0], refs[1], refs[2 : 2 + count]
    refs = refs[2 + count :]
    pair = refs[:count]
    middle = refs[count : 2 * count]
    line = refs[2 * count : 3 * count]
    far = refs[3 * count : 4 * count]
    flat_pair, flat_mid, flat_top, flat_group, send, receive, flat_send, flat_receive, sum_sems = (
        refs[4 * count :]
    )
    me, t, m, core = position(top, mid)
    group = lax.axis_index("seq")
    greet(groups, top, mid)
    other = {"fsdp": slot_of(t, m, 1 - core, mid)}
    to_mid = [{"fsdp": slot_of(t, lax.rem(m + e, mid), core, mid)} for e in range(mid)]
    to_top = [{"fsdp": slot_of(lax.rem(t + d, top), m, core, mid)} for d in range(top)]
    to_group = [{"seq": lax.rem(group + k, groups)} for k in range(groups)]
    copies = []

    def launch(source, target, index, device):
        copy = remote(source, target, send.at[index], receive.at[index], device)
        copies.append(copy)
        return copy

    def launch_flat(stage, buffer, own, peers):
        started = []
        for k in range(1, len(peers)):
            copy = remote(
                buffer.at[own],
                buffer.at[own],
                flat_send.at[stage, k],
                flat_receive.at[stage, k],
                peers[k],
            )
            started.append(copy)
            copies.append(copy)
        return started

    def total_of(buffer, started):
        for copy in started:
            copy.wait_recv()
        value = buffer[0]
        for k in range(1, buffer.shape[0]):
            value = value + buffer[k]
        return value

    work = [(a, r) for a in range(count) for r in range(CHUNKS)]
    rows_of = [grads[a].shape[3] // CHUNKS for a in range(count)]

    def part(a, r):
        return pl.ds(r * rows_of[a], rows_of[a])

    flat_pair[core] = flat[...]
    stage_flat = launch_flat(0, flat_pair, core, [None, other])
    stage = {}
    for n, (a, r) in enumerate(work):
        stage[n] = launch(
            grads[a].at[:, :, 1 - core, part(a, r)], pair[a].at[:, :, part(a, r)], (n, 0), other
        )
    sums = []
    for k in range(1, groups):
        copy = remote(
            partial.at[lax.rem(group + k, groups)],
            summed.at[group],
            sum_sems.at[0, k],
            sum_sems.at[1, k],
            to_group[k],
        )
        sums.append(copy)
    summed[group] = partial[group]

    stage_mid = {}
    for n, (a, r) in enumerate(work):
        stage[n].wait_recv()

        @pl.loop(0, top)
        def _(i):
            for j in range(mid):
                at = part(a, r)
                pair[a][i, j, at] = add(pair[a][i, j, at], grads[a][i, j, core, at])

        for e in range(1, mid):
            stage_mid[n, e] = launch(
                pair[a].at[:, lax.rem(m + e, mid), part(a, r)],
                middle[a].at[e - 1, :, part(a, r)],
                (n, e),
                to_mid[e],
            )
        if n == 0:
            flat_mid[m] = total_of(flat_pair, stage_flat)
            stage_flat = launch_flat(1, flat_mid, m, to_mid)
    stage_top = {}
    for n, (a, r) in enumerate(work):
        for e in range(1, mid):
            stage_mid[n, e].wait_recv()

        @pl.loop(0, top)
        def _(i):
            at = part(a, r)
            value = pair[a][i, m, at].astype(f32)
            for e in range(1, mid):
                value = value + middle[a][e - 1, i, at].astype(f32)
            line[a][i, at] = value.astype(bf16)

        for d in range(1, top):
            stage_top[n, d] = launch(
                line[a].at[lax.rem(t + d, top), part(a, r)],
                far[a].at[d - 1, part(a, r)],
                (n, mid + d - 1),
                to_top[d],
            )
        if n == 0:
            flat_top[t] = total_of(flat_mid, stage_flat)
            stage_flat = launch_flat(2, flat_top, t, to_top)
    last = []
    for n, (a, r) in enumerate(work):
        at = part(a, r)
        for d in range(1, top):
            stage_top[n, d].wait_recv()
        value = line[a][t, at].astype(f32)
        for d in range(1, top):
            value = value + far[a][d - 1, at].astype(f32)
        owned[a][group, at] = value.astype(bf16)
        for k in range(1, groups):
            last.append(
                launch(
                    owned[a].at[group, at],
                    owned[a].at[group, at],
                    (n, mid + top - 2 + k),
                    to_group[k],
                )
            )
        if n == 0:
            flat_group[group] = total_of(flat_top, stage_flat)
            stage_flat = launch_flat(3, flat_group, group, to_group)
    total[...] = total_of(flat_group, stage_flat)
    for copy in last:
        copy.wait_recv()
    for copy in sums:
        copy.wait()
    for copy in copies:
        copy.wait_send()


def scatter_all(groups, shards, partial, flat, grads):
    top, mid = factors(shards)
    count = len(grads)
    vmem = pl.BlockSpec(memory_space=pltpu.VMEM)
    grads = [grad.reshape(top, mid, 2, grad.shape[0] // shards, grad.shape[1]) for grad in grads]
    shapes = [grad.shape[3:] for grad in grads]
    out = [
        jax.ShapeDtypeStruct(partial.shape, bf16),
        jax.ShapeDtypeStruct(flat.shape, f32),
    ] + [jax.ShapeDtypeStruct((groups,) + shape, bf16) for shape in shapes]
    most = max(2, mid, top, groups)
    stages = mid + top + groups - 2
    return pl.pallas_call(
        functools.partial(scatter_kernel, groups, top, mid, count),
        out_shape=out,
        in_specs=[vmem] * (2 + count),
        out_specs=[vmem] * (2 + count),
        scratch_shapes=[pltpu.VMEM((top, mid) + shape, bf16) for shape in shapes]
        + [pltpu.VMEM((max(1, mid - 1), top) + shape, bf16) for shape in shapes]
        + [pltpu.VMEM((top,) + shape, bf16) for shape in shapes]
        + [pltpu.VMEM((max(1, top - 1),) + shape, bf16) for shape in shapes]
        + [pltpu.VMEM((size,) + flat.shape, f32) for size in (2, mid, top, groups)]
        + [
            pltpu.SemaphoreType.DMA((count * CHUNKS, stages)),
            pltpu.SemaphoreType.DMA((count * CHUNKS, stages)),
            pltpu.SemaphoreType.DMA((4, most)),
            pltpu.SemaphoreType.DMA((4, most)),
            pltpu.SemaphoreType.DMA((2, groups)),
        ],
        compiler_params=pltpu.CompilerParams(
            collective_id=1, has_side_effects=True, vmem_limit_bytes=VMEM_LIMIT
        ),
    )(partial, flat, *grads)


def local(
    tokens,
    cotangent,
    documents,
    in_weight,
    kernel_taps,
    kernel_bias,
    step_bias,
    decay_log,
    skip_gain,
    pre_gain,
    norm_gain,
    out_weight,
):
    groups = lax.axis_size("seq")
    shards = lax.axis_size("fsdp")
    group = lax.axis_index("seq")
    heads = step_bias.shape[0]
    inner = norm_gain.shape[0]
    states = kernel_bias.shape[0] - inner
    half = inner // groups
    spread = out_weight.shape[0] % (HEAD_DIM * groups) == 0
    parts = shards if spread else 1

    def pick(array, axis):
        size = array.shape[axis]
        lead, tail = array.shape[:axis], array.shape[axis + 1 :]
        split = array.reshape(lead + (parts, groups, size // (parts * groups)) + tail)
        chosen = lax.dynamic_index_in_dim(split, group, axis + 1, keepdims=False)
        return chosen.reshape(lead + (size // groups,) + tail)

    def place(array):
        size = array.shape[-1] * groups
        lead = array.shape[:-1]
        split = array.reshape(lead + (parts, 1, size // (parts * groups)))
        blank = jnp.zeros(lead + (parts, groups, size // (parts * groups)), array.dtype)
        full = lax.dynamic_update_slice_in_dim(blank, split, group, len(lead) + 1)
        return full.reshape(lead + (size,))

    def unite(array):
        rows, width = array.shape[1:]
        split = array.reshape(groups, rows, parts, width // parts)
        return split.transpose(1, 2, 0, 3).reshape(rows, width * groups)

    conv_end = inner + inner + states
    conv_shard = jnp.concatenate(
        [
            pick(in_weight[:, inner : 2 * inner], 1),
            in_weight[:, 2 * inner : conv_end],
            pick(in_weight[:, conv_end:], 1),
        ],
        axis=1,
    )
    gate_shard = pick(in_weight[:, :inner], 1)
    out_rows = out_weight
    if spread:
        split = out_weight.reshape(groups, out_weight.shape[0] // groups, out_weight.shape[1])
        out_rows = lax.dynamic_index_in_dim(split, group, 0, keepdims=False)
    floats = tokens.astype(f32)
    normed_own = pre_norm(floats, pre_gain).astype(bf16)
    count, width = tokens.shape
    joined, conv_weight, gate_weight, out_part = gather_all(
        groups,
        shards,
        jnp.concatenate([normed_own, cotangent], axis=1),
        [conv_shard, gate_shard, out_rows],
    )
    joined = joined.reshape(groups * count, 2 * width)
    conv_weight = conv_weight.reshape(width, -1)
    gate_weight = gate_weight.reshape(width, -1)
    out_part = out_part.reshape(-1, width)
    if not spread:
        out_part = lax.dynamic_slice_in_dim(out_part, group * half, half, 0)
    normed_in, cot = joined[:, :width], joined[:, width:]

    projected = dot(normed_in, conv_weight).astype(bf16).astype(f32)
    segment = documents[0]
    taps = jnp.concatenate([pick(kernel_taps[:, :inner], 1), kernel_taps[:, inner:]], axis=1)
    tap_bias = jnp.concatenate([pick(kernel_bias[:inner], 0), kernel_bias[inner:]], axis=0)
    mixed, mixer_back = jax.vjp(
        lambda *given: mixer(segment, *given),
        projected[:, : half + states],
        projected[:, half + states :],
        taps,
        tap_bias,
        pick(step_bias, 0),
        pick(decay_log, 0),
        pick(skip_gain, 0),
    )
    gain = pick(norm_gain, 0)
    gates = dot(normed_in, gate_weight).astype(bf16).astype(f32)
    mixed = mixed.astype(bf16).astype(f32)
    back_normed = dot(cot, out_part, contract_rows)
    sigmoid = jax.nn.sigmoid(gates)
    silu = gates * sigmoid
    gated = mixed * silu
    back_gain = back_normed * gain
    sums = lax.psum(
        jnp.stack([jnp.sum(gated * gated, axis=1), jnp.sum(gated * back_gain, axis=1)]), "seq"
    )
    scale = lax.rsqrt(sums[0] / inner + norm_epsilon)
    unit = gated * scale[:, None]
    normed_bf = (unit * gain).astype(bf16)
    norm_gain_part = jnp.sum(back_normed * unit, axis=0)
    back_gated = scale[:, None] * (back_gain - unit * (scale * sums[1] / inner)[:, None])
    back_mixed = (back_gated * silu).astype(bf16).astype(f32)
    back_gates = (back_gated * mixed * sigmoid * (1.0 + gates * (1.0 - sigmoid))).astype(bf16)

    outward = dot(normed_bf, cot, contract_tokens).astype(bf16)
    gate_grad = dot(normed_in, back_gates, contract_tokens).astype(bf16)
    if not spread:
        blank = jnp.zeros((inner, width), bf16)
        outward = lax.dynamic_update_slice_in_dim(blank, outward, group * half, 0)
    branch = dot(normed_bf, out_part).astype(bf16)

    back_conv, back_steps, taps_part, bias_part, step_part, decay_part, skip_part = mixer_back(
        back_mixed
    )
    back_projected = jnp.concatenate([back_conv, back_steps], axis=1).astype(bf16)
    conv_grad = dot(normed_in, back_projected, contract_tokens).astype(bf16)
    back_in = dot(back_projected, conv_weight, contract_rows) + dot(
        back_gates, gate_weight, contract_rows
    )
    pre_gain_part = jnp.sum(back_in * normed_in.astype(f32), axis=0) / pre_gain

    pieces = (
        jnp.concatenate([place(taps_part[:, :half]), taps_part[:, half:]], axis=1),
        jnp.concatenate([place(bias_part[:half]), bias_part[half:]], axis=0),
        place(step_part),
        place(decay_part),
        place(skip_part),
        pre_gain_part,
        place(norm_gain_part),
    )
    flat = jnp.concatenate([piece.reshape(-1) for piece in pieces])
    padded = jnp.pad(flat, (0, -flat.size % 1024)).reshape(-1, 128)
    partial = jnp.concatenate(
        [
            back_in.astype(bf16).reshape(groups, count, width),
            branch.reshape(groups, count, width),
        ],
        axis=1,
    )
    partial, padded, conv_all, gate_all, out_all = scatter_all(
        groups, shards, partial, padded, [conv_grad, gate_grad, outward]
    )
    partial = jnp.sum(partial.astype(f32), axis=0)
    block_output = (floats + partial[count:]).astype(bf16)
    _, pre_back = jax.vjp(lambda given: pre_norm(given, pre_gain), floats)
    tokens_grad = cotangent.astype(f32) + pre_back(partial[:count])[0]
    conv_all, gate_all, out_all = (
        conv_all.astype(f32),
        gate_all.astype(f32),
        out_all.astype(f32),
    )
    if spread:
        outward_grad = out_all.reshape(-1, width)
    else:
        outward_grad = jnp.sum(out_all, axis=0)
    inward_grad = jnp.concatenate(
        [
            unite(gate_all),
            unite(conv_all[:, :, :half]),
            jnp.sum(conv_all[:, :, half : half + states], axis=0),
            unite(conv_all[:, :, half + states :]),
        ],
        axis=1,
    )
    flat = padded.reshape(-1)
    totals = []
    start = 0
    for piece in pieces:
        totals.append(flat[start : start + piece.size].reshape(piece.shape))
        start += piece.size
    return (
        block_output,
        tokens_grad,
        inward_grad,
        totals[0],
        totals[1],
        totals[2],
        totals[3],
        totals[4],
        totals[5],
        totals[6],
        outward_grad,
    )


def solution(mesh):
    rows = P(("fsdp", "seq"), None)
    split = P("fsdp", None)
    return jax.shard_map(
        local,
        mesh=mesh,
        in_specs=(rows, rows, split, split) + (P(),) * 7 + (split,),
        out_specs=(rows, rows, split) + (P(),) * 7 + (split,),
        check_vma=False,
    )
```

```python
import functools
import math

import jax
import jax.numpy as jnp
from jax import lax
from jax.experimental import pallas as pl
from jax.experimental.pallas import tpu as pltpu
from jax.sharding import PartitionSpec as P

HEAD_DIM = 64
STATE = 128
CONV = 4
SPAN = 256

norm_epsilon = 1e-05
bf16 = jnp.bfloat16
f32 = jnp.float32
contract_rows = (((1,), (1,)), ((), ()))
contract_tokens = (((0,), (0,)), ((), ()))


def dot(left, right, dims=(((1,), (0,)), ((), ()))):
    return lax.dot_general(left, right, dims, preferred_element_type=f32)


def pre_norm(values, gain):
    scale = lax.rsqrt(jnp.mean(values * values, axis=-1, keepdims=True) + norm_epsilon)
    return values * scale * gain


def product(spec, left, right):
    return jnp.einsum(spec, left.astype(bf16), right.astype(bf16), preferred_element_type=f32)


def mixer(segment, conv_in, step_raw, taps, tap_bias, bias_steps, log_rates, skips):
    length, channels = conv_in.shape
    heads = step_raw.shape[1]
    width = heads * HEAD_DIM
    spots = jnp.arange(length)
    same = segment[:, None] == segment[None, :]
    gap = spots[:, None] - spots[None, :]
    moves = jnp.concatenate(
        [((gap == offset) & same).astype(bf16) for offset in range(1, CONV)], axis=0
    )
    moved = jnp.dot(moves, conv_in.astype(bf16), preferred_element_type=bf16)
    summed = tap_bias + conv_in * taps[CONV - 1]
    for offset in range(1, CONV):
        shifted = moved[(offset - 1) * length : offset * length].astype(f32)
        summed = summed + taps[CONV - 1 - offset] * shifted
    active = jax.nn.silu(summed)
    values = active[:, :width].reshape(length, heads, HEAD_DIM).transpose(1, 0, 2)
    input_matrix = active[:, width : width + STATE]
    output_matrix = active[:, width + STATE :]
    steps_taken = jax.nn.softplus(step_raw + bias_steps)
    log_decay = (steps_taken * -jnp.exp(log_rates)).T
    scaled = values * steps_taken.T[:, :, None]
    span = min(SPAN, length)
    blocks = length // span
    places = jnp.arange(span)
    state = None
    outputs = []
    for block in range(blocks):
        at = slice(block * span, (block + 1) * span)
        seg = segment[at]
        cumul = jnp.cumsum(log_decay[:, at], axis=1)
        causal = (places[:, None] >= places[None, :]) & (seg[:, None] == seg[None, :])
        log_gap = cumul[:, :, None] - cumul[:, None, :]
        decay = jnp.where(causal[None], jnp.exp(jnp.where(causal[None], log_gap, 0.0)), 0.0)
        scores = product("in,jn->ij", output_matrix[at], input_matrix[at])
        inside = product("hij,hjp->hip", decay * scores[None], scaled[:, at])
        if state is not None:
            previous = segment[block * span - 1]
            entering = jnp.exp(cumul) * (seg == previous).astype(f32)[None]
            inside = inside + product("in,hnp->hip", output_matrix[at], state) * entering[:, :, None]
        if block + 1 < blocks:
            final = cumul[:, -1]
            leaving = jnp.exp(final[:, None] - cumul) * (seg == seg[-1]).astype(f32)[None]
            fresh = product("jn,hjp->hnp", input_matrix[at], scaled[:, at] * leaving[:, :, None])
            if state is None:
                state = fresh
            else:
                keeping = jnp.exp(final) * (seg[-1] == previous).astype(f32)
                state = keeping[:, None, None] * state + fresh
        outputs.append(inside)
    whole = outputs[0] if blocks == 1 else jnp.concatenate(outputs, axis=1)
    result = whole + values * skips[:, None, None]
    return result.transpose(1, 0, 2).reshape(length, width)

MESH = pl.DeviceIdType.MESH
VMEM_LIMIT = 60 * 1024 * 1024


def factors(shards):
    rest = shards // 2
    mid = 1 << (int(math.log2(rest)) // 2)
    return rest // mid, mid


def position(top, mid):
    me = lax.axis_index("fsdp")
    return me, me // (2 * mid), lax.rem(me // 2, mid), lax.rem(me, 2)


def slot_of(t, m, core, mid):
    return (t * mid + m) * 2 + core


def greet(groups, top, mid):
    me, t, m, core = position(top, mid)
    group = lax.axis_index("seq")
    peers = [{"fsdp": slot_of(lax.rem(t + d, top), m, core, mid)} for d in range(1, top)]
    peers += [{"fsdp": slot_of(t, lax.rem(m + e, mid), core, mid)} for e in range(1, mid)]
    peers += [{"fsdp": slot_of(t, m, 1 - core, mid)}]
    peers += [{"seq": lax.rem(group + k, groups)} for k in range(1, groups)]
    barrier = pltpu.get_barrier_semaphore()
    for peer in peers:
        pl.semaphore_signal(barrier, inc=1, device_id=peer, device_id_type=MESH)
    pl.semaphore_wait(barrier, len(peers))


def remote(source, target, send, receive, device):
    copy = pltpu.make_async_remote_copy(
        src_ref=source,
        dst_ref=target,
        send_sem=send,
        recv_sem=receive,
        device_id=device,
        device_id_type=MESH,
    )
    copy.start()
    return copy


def gather_kernel(groups, top, mid, count, *refs):
    rows, shards = refs[0], refs[1 : 1 + count]
    all_rows, wholes = refs[1 + count], refs[2 + count : 2 + 2 * count]
    send, receive, row_send, row_receive = refs[2 + 2 * count :]
    me, t, m, core = position(top, mid)
    group = lax.axis_index("seq")
    greet(groups, top, mid)
    copies = {}

    def launch(a, key, source, slot, device):
        copies[(a,) + key] = remote(
            source, wholes[a].at[slot], send.at[(a,) + key], receive.at[(a,) + key], device
        )

    other = {"fsdp": slot_of(t, m, 1 - core, mid)}
    for a in range(count):
        for d in range(1, top):
            peer = {"fsdp": slot_of(lax.rem(t + d, top), m, core, mid)}
            launch(a, (d, 0, 0), shards[a], me, peer)
        for e in range(1, mid):
            peer = {"fsdp": slot_of(t, lax.rem(m + e, mid), core, mid)}
            launch(a, (0, e, 0), shards[a], me, peer)
        launch(a, (0, 0, 1), shards[a], me, other)
    for k in range(1, groups):
        copies[("rows", k)] = remote(
            rows,
            all_rows.at[group],
            row_send.at[k],
            row_receive.at[k],
            {"seq": lax.rem(group + k, groups)},
        )
    for a in range(count):
        wholes[a][me] = shards[a][...]
    all_rows[group] = rows[...]
    for a in range(count):
        for d in range(1, top):
            copies[(a, d, 0, 0)].wait_recv()
            slot = slot_of(lax.rem(t - d + top, top), m, core, mid)
            for e in range(1, mid):
                peer = {"fsdp": slot_of(t, lax.rem(m + e, mid), core, mid)}
                launch(a, (d, e, 0), wholes[a].at[slot], slot, peer)
            launch(a, (d, 0, 1), wholes[a].at[slot], slot, other)
    for a in range(count):
        for d in range(top):
            for e in range(1, mid):
                copies[(a, d, e, 0)].wait_recv()
                slot = slot_of(lax.rem(t - d + top, top), lax.rem(m - e + mid, mid), core, mid)
                launch(a, (d, e, 1), wholes[a].at[slot], slot, other)
    for key, copy in copies.items():
        copy.wait_send()
        if key[0] == "rows" or key[3] == 1:
            copy.wait_recv()


def gather_all(groups, shards, rows, arrays):
    top, mid = factors(shards)
    count = len(arrays)
    vmem = pl.BlockSpec(memory_space=pltpu.VMEM)
    out = [jax.ShapeDtypeStruct((groups,) + rows.shape, rows.dtype)]
    out += [jax.ShapeDtypeStruct((shards,) + array.shape, array.dtype) for array in arrays]
    return pl.pallas_call(
        functools.partial(gather_kernel, groups, top, mid, count),
        out_shape=out,
        in_specs=[vmem] * (1 + count),
        out_specs=[vmem] * (1 + count),
        scratch_shapes=[
            pltpu.SemaphoreType.DMA((count, top, mid, 2)),
            pltpu.SemaphoreType.DMA((count, top, mid, 2)),
            pltpu.SemaphoreType.DMA((groups,)),
            pltpu.SemaphoreType.DMA((groups,)),
        ],
        compiler_params=pltpu.CompilerParams(
            collective_id=0, has_side_effects=True, vmem_limit_bytes=VMEM_LIMIT
        ),
    )(rows, *arrays)


CHUNKS = 2


def add(left, right):
    return (left.astype(f32) + right.astype(f32)).astype(bf16)


def scatter_kernel(groups, top, mid, count, *refs):
    partial, flat, grads = refs[0], refs[1], refs[2 : 2 + count]
    refs = refs[2 + count :]
    summed, total, owned = refs[0], refs[1], refs[2 : 2 + count]
    refs = refs[2 + count :]
    pair = refs[:count]
    middle = refs[count : 2 * count]
    line = refs[2 * count : 3 * count]
    far = refs[3 * count : 4 * count]
    flat_pair, flat_mid, flat_top, flat_group, send, receive, flat_send, flat_receive, sum_sems = (
        refs[4 * count :]
    )
    me, t, m, core = position(top, mid)
    group = lax.axis_index("seq")
    greet(groups, top, mid)
    other = {"fsdp": slot_of(t, m, 1 - core, mid)}
    to_mid = [{"fsdp": slot_of(t, lax.rem(m + e, mid), core, mid)} for e in range(mid)]
    to_top = [{"fsdp": slot_of(lax.rem(t + d, top), m, core, mid)} for d in range(top)]
    to_group = [{"seq": lax.rem(group + k, groups)} for k in range(groups)]
    copies = []

    def launch(source, target, index, device):
        copy = remote(source, target, send.at[index], receive.at[index], device)
        copies.append(copy)
        return copy

    def launch_flat(stage, buffer, own, peers):
        started = []
        for k in range(1, len(peers)):
            copy = remote(
                buffer.at[own],
                buffer.at[own],
                flat_send.at[stage, k],
                flat_receive.at[stage, k],
                peers[k],
            )
            started.append(copy)
            copies.append(copy)
        return started

    def total_of(buffer, started):
        for copy in started:
            copy.wait_recv()
        value = buffer[0]
        for k in range(1, buffer.shape[0]):
            value = value + buffer[k]
        return value

    work = [(a, r) for a in range(count) for r in range(CHUNKS)]
    rows_of = [grads[a].shape[3] // CHUNKS for a in range(count)]

    def part(a, r):
        return pl.ds(r * rows_of[a], rows_of[a])

    flat_pair[core] = flat[...]
    stage_flat = launch_flat(0, flat_pair, core, [None, other])
    stage = {}
    for n, (a, r) in enumerate(work):
        stage[n] = launch(
            grads[a].at[:, :, 1 - core, part(a, r)], pair[a].at[:, :, part(a, r)], (n, 0), other
        )
    sums = []
    for k in range(1, groups):
        copy = remote(
            partial.at[lax.rem(group + k, groups)],
            summed.at[group],
            sum_sems.at[0, k],
            sum_sems.at[1, k],
            to_group[k],
        )
        sums.append(copy)
    summed[group] = partial[group]

    stage_mid = {}
    for n, (a, r) in enumerate(work):
        stage[n].wait_recv()

        @pl.loop(0, top)
        def _(i):
            for j in range(mid):
                at = part(a, r)
                pair[a][i, j, at] = add(pair[a][i, j, at], grads[a][i, j, core, at])

        for e in range(1, mid):
            stage_mid[n, e] = launch(
                pair[a].at[:, lax.rem(m + e, mid), part(a, r)],
                middle[a].at[e - 1, :, part(a, r)],
                (n, e),
                to_mid[e],
            )
        if n == 0:
            flat_mid[m] = total_of(flat_pair, stage_flat)
            stage_flat = launch_flat(1, flat_mid, m, to_mid)
    stage_top = {}
    for n, (a, r) in enumerate(work):
        for e in range(1, mid):
            stage_mid[n, e].wait_recv()

        @pl.loop(0, top)
        def _(i):
            at = part(a, r)
            value = pair[a][i, m, at].astype(f32)
            for e in range(1, mid):
                value = value + middle[a][e - 1, i, at].astype(f32)
            line[a][i, at] = value.astype(bf16)

        for d in range(1, top):
            stage_top[n, d] = launch(
                line[a].at[lax.rem(t + d, top), part(a, r)],
                far[a].at[d - 1, part(a, r)],
                (n, mid + d - 1),
                to_top[d],
            )
        if n == 0:
            flat_top[t] = total_of(flat_mid, stage_flat)
            stage_flat = launch_flat(2, flat_top, t, to_top)
    last = []
    for n, (a, r) in enumerate(work):
        at = part(a, r)
        for d in range(1, top):
            stage_top[n, d].wait_recv()
        value = line[a][t, at].astype(f32)
        for d in range(1, top):
            value = value + far[a][d - 1, at].astype(f32)
        owned[a][group, at] = value.astype(bf16)
        for k in range(1, groups):
            last.append(
                launch(
                    owned[a].at[group, at],
                    owned[a].at[group, at],
                    (n, mid + top - 2 + k),
                    to_group[k],
                )
            )
        if n == 0:
            flat_group[group] = total_of(flat_top, stage_flat)
            stage_flat = launch_flat(3, flat_group, group, to_group)
    total[...] = total_of(flat_group, stage_flat)
    for copy in last:
        copy.wait_recv()
    for copy in sums:
        copy.wait()
    for copy in copies:
        copy.wait_send()


def scatter_all(groups, shards, partial, flat, grads):
    top, mid = factors(shards)
    count = len(grads)
    vmem = pl.BlockSpec(memory_space=pltpu.VMEM)
    grads = [grad.reshape(top, mid, 2, grad.shape[0] // shards, grad.shape[1]) for grad in grads]
    shapes = [grad.shape[3:] for grad in grads]
    out = [
        jax.ShapeDtypeStruct(partial.shape, bf16),
        jax.ShapeDtypeStruct(flat.shape, f32),
    ] + [jax.ShapeDtypeStruct((groups,) + shape, bf16) for shape in shapes]
    most = max(2, mid, top, groups)
    stages = mid + top + groups - 2
    return pl.pallas_call(
        functools.partial(scatter_kernel, groups, top, mid, count),
        out_shape=out,
        in_specs=[vmem] * (2 + count),
        out_specs=[vmem] * (2 + count),
        scratch_shapes=[pltpu.VMEM((top, mid) + shape, bf16) for shape in shapes]
        + [pltpu.VMEM((max(1, mid - 1), top) + shape, bf16) for shape in shapes]
        + [pltpu.VMEM((top,) + shape, bf16) for shape in shapes]
        + [pltpu.VMEM((max(1, top - 1),) + shape, bf16) for shape in shapes]
        + [pltpu.VMEM((size,) + flat.shape, f32) for size in (2, mid, top, groups)]
        + [
            pltpu.SemaphoreType.DMA((count * CHUNKS, stages)),
            pltpu.SemaphoreType.DMA((count * CHUNKS, stages)),
            pltpu.SemaphoreType.DMA((4, most)),
            pltpu.SemaphoreType.DMA((4, most)),
            pltpu.SemaphoreType.DMA((2, groups)),
        ],
        compiler_params=pltpu.CompilerParams(
            collective_id=1, has_side_effects=True, vmem_limit_bytes=VMEM_LIMIT
        ),
    )(partial, flat, *grads)


def local(
    tokens,
    cotangent,
    documents,
    in_weight,
    kernel_taps,
    kernel_bias,
    step_bias,
    decay_log,
    skip_gain,
    pre_gain,
    norm_gain,
    out_weight,
):
    groups = lax.axis_size("seq")
    shards = lax.axis_size("fsdp")
    group = lax.axis_index("seq")
    heads = step_bias.shape[0]
    inner = norm_gain.shape[0]
    states = kernel_bias.shape[0] - inner
    half = inner // groups
    spread = out_weight.shape[0] % (HEAD_DIM * groups) == 0
    parts = shards if spread else 1

    def pick(array, axis):
        size = array.shape[axis]
        lead, tail = array.shape[:axis], array.shape[axis + 1 :]
        split = array.reshape(lead + (parts, groups, size // (parts * groups)) + tail)
        chosen = lax.dynamic_index_in_dim(split, group, axis + 1, keepdims=False)
        return chosen.reshape(lead + (size // groups,) + tail)

    def place(array):
        size = array.shape[-1] * groups
        lead = array.shape[:-1]
        split = array.reshape(lead + (parts, 1, size // (parts * groups)))
        blank = jnp.zeros(lead + (parts, groups, size // (parts * groups)), array.dtype)
        full = lax.dynamic_update_slice_in_dim(blank, split, group, len(lead) + 1)
        return full.reshape(lead + (size,))

    def unite(array):
        rows, width = array.shape[1:]
        split = array.reshape(groups, rows, parts, width // parts)
        return split.transpose(1, 2, 0, 3).reshape(rows, width * groups)

    conv_end = inner + inner + states
    conv_shard = jnp.concatenate(
        [
            pick(in_weight[:, inner : 2 * inner], 1),
            in_weight[:, 2 * inner : conv_end],
            pick(in_weight[:, conv_end:], 1),
        ],
        axis=1,
    )
    gate_shard = pick(in_weight[:, :inner], 1)
    out_rows = out_weight
    if spread:
        split = out_weight.reshape(groups, out_weight.shape[0] // groups, out_weight.shape[1])
        out_rows = lax.dynamic_index_in_dim(split, group, 0, keepdims=False)
    floats = tokens.astype(f32)
    normed_own = pre_norm(floats, pre_gain).astype(bf16)
    count, width = tokens.shape
    joined, conv_weight, gate_weight, out_part = gather_all(
        groups,
        shards,
        jnp.concatenate([normed_own, cotangent], axis=1),
        [conv_shard, gate_shard, out_rows],
    )
    joined = joined.reshape(groups * count, 2 * width)
    conv_weight = conv_weight.reshape(width, -1)
    gate_weight = gate_weight.reshape(width, -1)
    out_part = out_part.reshape(-1, width)
    if not spread:
        out_part = lax.dynamic_slice_in_dim(out_part, group * half, half, 0)
    normed_in, cot = joined[:, :width], joined[:, width:]

    projected = dot(normed_in, conv_weight).astype(bf16).astype(f32)
    segment = documents[0]
    taps = jnp.concatenate([pick(kernel_taps[:, :inner], 1), kernel_taps[:, inner:]], axis=1)
    tap_bias = jnp.concatenate([pick(kernel_bias[:inner], 0), kernel_bias[inner:]], axis=0)
    mixed, mixer_back = jax.vjp(
        lambda *given: mixer(segment, *given),
        projected[:, : half + states],
        projected[:, half + states :],
        taps,
        tap_bias,
        pick(step_bias, 0),
        pick(decay_log, 0),
        pick(skip_gain, 0),
    )
    gain = pick(norm_gain, 0)
    gates = dot(normed_in, gate_weight).astype(bf16).astype(f32)
    mixed = mixed.astype(bf16).astype(f32)
    back_normed = dot(cot, out_part, contract_rows)
    sigmoid = jax.nn.sigmoid(gates)
    silu = gates * sigmoid
    gated = mixed * silu
    back_gain = back_normed * gain
    sums = lax.psum(
        jnp.stack([jnp.sum(gated * gated, axis=1), jnp.sum(gated * back_gain, axis=1)]), "seq"
    )
    scale = lax.rsqrt(sums[0] / inner + norm_epsilon)
    unit = gated * scale[:, None]
    normed_bf = (unit * gain).astype(bf16)
    norm_gain_part = jnp.sum(back_normed * unit, axis=0)
    back_gated = scale[:, None] * (back_gain - unit * (scale * sums[1] / inner)[:, None])
    back_mixed = (back_gated * silu).astype(bf16).astype(f32)
    back_gates = (back_gated * mixed * sigmoid * (1.0 + gates * (1.0 - sigmoid))).astype(bf16)

    outward = dot(normed_bf, cot, contract_tokens).astype(bf16)
    gate_grad = dot(normed_in, back_gates, contract_tokens).astype(bf16)
    if not spread:
        blank = jnp.zeros((inner, width), bf16)
        outward = lax.dynamic_update_slice_in_dim(blank, outward, group * half, 0)
    branch = dot(normed_bf, out_part).astype(bf16)

    back_conv, back_steps, taps_part, bias_part, step_part, decay_part, skip_part = mixer_back(
        back_mixed
    )
    back_projected = jnp.concatenate([back_conv, back_steps], axis=1).astype(bf16)
    conv_grad = dot(normed_in, back_projected, contract_tokens).astype(bf16)
    back_in = dot(back_projected, conv_weight, contract_rows) + dot(
        back_gates, gate_weight, contract_rows
    )
    pre_gain_part = jnp.sum(back_in * normed_in.astype(f32), axis=0) / pre_gain

    pieces = (
        jnp.concatenate([place(taps_part[:, :half]), taps_part[:, half:]], axis=1),
        jnp.concatenate([place(bias_part[:half]), bias_part[half:]], axis=0),
        place(step_part),
        place(decay_part),
        place(skip_part),
        pre_gain_part,
        place(norm_gain_part),
    )
    flat = jnp.concatenate([piece.reshape(-1) for piece in pieces])
    padded = jnp.pad(flat, (0, -flat.size % 1024)).reshape(-1, 128)
    partial = jnp.concatenate(
        [
            back_in.astype(bf16).reshape(groups, count, width),
            branch.reshape(groups, count, width),
        ],
        axis=1,
    )
    partial, padded, conv_all, gate_all, out_all = scatter_all(
        groups, shards, partial, padded, [conv_grad, gate_grad, outward]
    )
    partial = jnp.sum(partial.astype(f32), axis=0)
    block_output = (floats + partial[count:]).astype(bf16)
    _, pre_back = jax.vjp(lambda given: pre_norm(given, pre_gain), floats)
    tokens_grad = cotangent.astype(f32) + pre_back(partial[:count])[0]
    conv_all, gate_all, out_all = (
        conv_all.astype(f32),
        gate_all.astype(f32),
        out_all.astype(f32),
    )
    if spread:
        outward_grad = out_all.reshape(-1, width)
    else:
        outward_grad = jnp.sum(out_all, axis=0)
    inward_grad = jnp.concatenate(
        [
            unite(gate_all),
            unite(conv_all[:, :, :half]),
            jnp.sum(conv_all[:, :, half : half + states], axis=0),
            unite(conv_all[:, :, half + states :]),
        ],
        axis=1,
    )
    flat = padded.reshape(-1)
    totals = []
    start = 0
    for piece in pieces:
        totals.append(flat[start : start + piece.size].reshape(piece.shape))
        start += piece.size
    return (
        block_output,
        tokens_grad,
        inward_grad,
        totals[0],
        totals[1],
        totals[2],
        totals[3],
        totals[4],
        totals[5],
        totals[6],
        outward_grad,
    )


def solution(mesh):
    rows = P(("fsdp", "seq"), None)
    split = P("fsdp", None)
    return jax.shard_map(
        local,
        mesh=mesh,
        in_specs=(rows, rows, split, split) + (P(),) * 7 + (split,),
        out_specs=(rows, rows, split) + (P(),) * 7 + (split,),
        check_vma=False,
    )
```
